512 devices in a mesh: channel: 16 (over z_hi, x), tm: 4 (over y), beam: 8 (over z_lo, core).
Axes of the slice: x: 4, y: 4, z: 16 (z_hi: 4, z_lo: 4; z = z_hi * 4 + z_lo), core: 2. Of those that a mesh axis runs over, the one named last changes fastest.
Arguments:
- voltages: bfloat16 [2, 2048, 64, 1024], P(None, ('beam', 'channel'), None, 'tm'), may hold values from -6 to 6
- positions: int32 [2048], replicated, may hold values from 0 to 1023
- delays: int32 [128, 1024], P(None, 'channel'), may hold values from 0 to 63
Outputs:
- intensity: float32 [1024, 64, 1024], P(('beam', 'tm'), 'channel')
- dedispersed: float32 [1024, 128, 64], P(('beam', 'tm'), 'channel')
The draws below stay inside these ranges and needn't reach their ends.
Inputs may be any that keep to these rules, and one draw needn't show every extreme that they name: `positions`: place on a grid of 4 cylinders by 256 places along each.
All inputs are finite; a program needn't handle non-finite values.
Results may differ from the reference program's by a relative error of at most 0.0071.
Values may be sent and summed in bfloat16 or wider, within the bound.
A program may use at most 64 MiB of HBM per device.

```python
import math
import jax
import jax.numpy as jnp
from jax import lax

FEEDS = 2048
CHANNELS = 64
BEAMS = 1024
UPCH = 16
TAPS = 8
SAMPLES = 1024
FRAMES = 64
FINE = 1024
DM = 128


def touch_ends(array, rng, low, high):
    shape = array.shape
    place = [jax.random.randint(jax.random.fold_in(rng, axis), (), 0, shape[axis]) for axis in range(len(shape))]
    array = array.at[tuple(place)].set(low)
    longest = shape.index(max(shape))
    place[longest] = (place[longest] + 1) % shape[longest]
    return array.at[tuple(place)].set(high)


def levels(stream_key, extent, pieces, smallest, largest):
    def one(position, parts):
        steps = jax.random.uniform(jax.random.fold_in(jax.random.fold_in(stream_key, 6), position), (parts,), jnp.float32, smallest / len(pieces), largest / len(pieces))
        return jnp.repeat(jnp.exp(steps), extent[position] // parts).reshape((-1,) + (1,) * (len(extent) - position - 1))

    gain = one(*pieces[0])
    for cut in pieces[1:]:
        gain = gain * one(*cut)
    return gain


def gaussian(stream_key, dims, deviation, bound, pieces=(), held_as=jnp.bfloat16):
    entries = deviation * jax.random.normal(stream_key, dims, jnp.float32)
    if pieces:
        entries = entries * levels(stream_key, dims, pieces, -0.22, 0.18)
    return jnp.clip(entries, -bound, bound).astype(held_as)


def setup_inputs(seed: int = 0) -> dict:
    streams_of = jax.random.split(jax.random.key(seed), 4)
    voltages = gaussian(streams_of[0], (2, FEEDS, CHANNELS, SAMPLES), 1.0, 6.0, ((1, 128), (3, 4)))
    positions = touch_ends(jax.random.randint(streams_of[1], (FEEDS,), 0, BEAMS), jax.random.fold_in(streams_of[1], 1), 0, BEAMS - 1).astype(jnp.int32)
    delays = touch_ends(jax.random.randint(streams_of[2], (DM, FINE), 0, FRAMES), jax.random.fold_in(streams_of[2], 1), 0, FRAMES - 1).astype(jnp.int32)
    return {"voltages": voltages, "positions": positions, "delays": delays}


TWO_PI = 2.0 * math.pi
HIGHEST = lax.Precision.HIGHEST

def window_table(tap_count, upch_factor):
    length = tap_count * upch_factor
    sample_index = jnp.arange(length).astype(jnp.float32)
    taper = jnp.sinc((sample_index - (length - 1) / 2.0) / upch_factor) * (0.5 - 0.5 * jnp.cos(TWO_PI * (sample_index + 0.5) / length))
    taper = taper / jnp.sqrt(jnp.sum(taper * taper))
    return taper.reshape(tap_count, upch_factor)

def steering(positions, beam_start, item_count, places, feed_count):
    beam_ids = beam_start + jnp.arange(item_count).astype(jnp.int32)
    beam_east = beam_ids // places
    beam_north = beam_ids % places
    cylinder = positions // places
    along_row = positions % places
    coarse = beam_east[:, None] * cylinder[None, :] % 4
    north_turns = beam_north[:, None] * along_row[None, :] % places
    angles = TWO_PI * (coarse.astype(jnp.float32) / 4.0 + north_turns.astype(jnp.float32) / places)
    norm_scale = 1.0 / math.sqrt(feed_count)
    w_real = (jnp.cos(angles) * norm_scale).astype(jnp.bfloat16)
    w_imag = (-jnp.sin(angles) * norm_scale).astype(jnp.bfloat16)
    top_half = jnp.concatenate([w_real, -w_imag], axis=1)
    low_half = jnp.concatenate([w_imag, w_real], axis=1)
    return jnp.concatenate([top_half, low_half], axis=0)

def reference(voltages, positions, delays):
    feed_count = voltages.shape[1]
    sample_count = voltages.shape[3]
    frame_count = sample_count // UPCH
    places = BEAMS // 4
    rim_width = (TAPS - 1) * UPCH
    weights = steering(positions, 0, BEAMS, places, feed_count)
    window = window_table(TAPS, UPCH)
    indices = jnp.arange(UPCH).astype(jnp.int32)
    phases = (indices[:, None] * indices[None, :] % UPCH).astype(jnp.float32) * (TWO_PI / UPCH)
    dft_real = jnp.cos(phases)
    dft_imag = -jnp.sin(phases)

    def channel_power(channel_data):
        stacked = channel_data.reshape(2 * feed_count, sample_count)
        formed = jnp.dot(weights, stacked, preferred_element_type=jnp.float32).astype(jnp.bfloat16)
        formed = formed.reshape(2, BEAMS, sample_count)
        padded = jnp.concatenate([jnp.zeros((2, BEAMS, rim_width), jnp.bfloat16), formed], axis=2)
        filtered = jnp.zeros((2, BEAMS, sample_count), jnp.float32)
        for tap_index in range(TAPS):
            filtered = filtered + padded[:, :, tap_index * UPCH:tap_index * UPCH + sample_count] * jnp.tile(window[tap_index], frame_count)
        halves = filtered.reshape(2, BEAMS, frame_count, UPCH)
        spec_real = jnp.einsum('bnm,mk->bnk', halves[0], dft_real, precision=HIGHEST) - jnp.einsum('bnm,mk->bnk', halves[1], dft_imag, precision=HIGHEST)
        spec_imag = jnp.einsum('bnm,mk->bnk', halves[0], dft_imag, precision=HIGHEST) + jnp.einsum('bnm,mk->bnk', halves[1], dft_real, precision=HIGHEST)
        return (spec_real * spec_real + spec_imag * spec_imag).reshape(BEAMS, sample_count)
    power_grid = lax.map(channel_power, jnp.moveaxis(voltages, 2, 0))
    intensity = jnp.transpose(power_grid, (1, 0, 2))
    frame_grid = intensity.reshape(BEAMS, CHANNELS, frame_count, UPCH)
    centred = frame_grid - lax.optimization_barrier(jnp.mean(frame_grid, axis=2, keepdims=True))
    spectrum = jnp.fft.rfft(centred, axis=2)
    freq_bins = frame_count // 2 + 1
    left_real = jnp.transpose(jnp.real(spectrum), (2, 0, 1, 3)).reshape(freq_bins, BEAMS, FINE)
    left_imag = jnp.transpose(jnp.imag(spectrum), (2, 0, 1, 3)).reshape(freq_bins, BEAMS, FINE)
    delay_cols = jnp.transpose(delays)

    def trial_bin(bin_data):
        frequency, part_real, part_imag = bin_data
        angle_grid = (frequency * delay_cols % frame_count).astype(jnp.float32) * (TWO_PI / frame_count)
        cos_table = jnp.cos(angle_grid)
        sin_table = jnp.sin(angle_grid)
        out_real = jnp.dot(part_real, cos_table, precision=HIGHEST) + jnp.dot(part_imag, sin_table, precision=HIGHEST)
        out_imag = jnp.dot(part_imag, cos_table, precision=HIGHEST) - jnp.dot(part_real, sin_table, precision=HIGHEST)
        return (out_real, out_imag)
    trial_real, trial_imag = lax.map(trial_bin, (jnp.arange(freq_bins).astype(jnp.int32), left_real, left_imag))
    series = jnp.fft.irfft(trial_real + 1j * trial_imag, n=frame_count, axis=0)
    dedispersed = jnp.transpose(series, (1, 2, 0)) / math.sqrt(FINE)
    return (intensity, dedispersed)
```

```python
import functools
import math

import jax
import jax.numpy as jnp
import numpy as np
from jax import lax
from jax.experimental import pallas as pl
from jax.experimental.pallas import tpu as pltpu
from jax.sharding import Mesh
from jax.sharding import PartitionSpec as P

F32 = jnp.float32
BF16 = jnp.bfloat16
FEEDS = 2048
TAPS = 8
UPCH = 16
FRAMES = 64
FINE = 1024


def cos_turns(steps, period):
    left = (steps & (period - 1)) - period // 2
    u = jnp.abs(left).astype(F32) * (4.0 / period) - 1.0
    u2 = u * u
    p = -3.598843235e-06
    for c in (1.604411848e-04, -4.681754135e-03, 7.969262625e-02, -6.459640975e-01, 1.570796327e00):
        p = p * u2 + c
    return p * u


def split(value):
    high = value.astype(BF16)
    return high, (value - high.astype(F32)).astype(BF16)


def mm(a, b):
    return jnp.dot(a, b, preferred_element_type=F32)


def table_split(table):
    table = jnp.asarray(table.astype(np.float32))
    high = table.astype(BF16)
    return high, (table - high.astype(F32)).astype(BF16)


def north_table():
    n = np.arange(256)
    angle = 2 * np.pi * (n[:, None] * n[None, :] % 256) / 256
    return np.concatenate([np.cos(angle), np.sin(angle)], axis=1) / math.sqrt(FEEDS)


def filter_table():
    length = TAPS * UPCH
    j = np.arange(length)
    h = np.sinc((j - (length - 1) / 2) / UPCH) * (0.5 - 0.5 * np.cos(2 * np.pi * (j + 0.5) / length))
    h = h / np.sqrt(np.sum(h * h))
    s = np.arange(256)
    out = np.arange(128)
    tap = (s[:, None] // 16 - 8) - out[None, :] // 16 + 7
    m = s % 16
    used = (tap >= 0) & (tap < 8)
    weight = np.where(used, h[np.clip(tap, 0, 7) * 16 + m[:, None]], 0.0)
    angle = 2 * np.pi * (m[:, None] * (out % 16)[None, :] % 16) / 16
    c = (weight * np.cos(angle)).reshape(2, 128, 128)
    d = (weight * np.sin(angle)).reshape(2, 128, 128)
    real_in = np.concatenate([c, -d], axis=2)
    imag_in = np.concatenate([d, c], axis=2)
    return np.stack([real_in, imag_in], axis=1).reshape(512, 256)


def relayout(v_ref, s_ref):
    for g in range(8):
        for h in range(2):
            x = v_ref[:, :, g * 8 : g * 8 + 8, h * 128 : h * 128 + 128]
            x = x.astype(F32).reshape(32, 8, 128)
            y = jnp.swapaxes(x, 0, 1).astype(BF16)
            for c in range(8):
                s_ref[(g * 8 + c) * 2 + h] = y[c]


def fill_places(pos_ref, oh_ref):
    pos = pos_ref[...]

    def body(i, carry):
        row = lax.broadcasted_iota(jnp.int32, (128, FEEDS), 0) + i * 128
        hit = jnp.where(row == pos, 1.0, 0.0).astype(BF16)
        oh_ref[pl.ds(pl.multiple_of(i * 128, 128), 128), :] = hit
        return carry

    lax.fori_loop(0, 8, body, 0)


def beamform(oh_ref, r1_ref, a_hi_ref, a_lo_ref, b_ref):
    xr = r1_ref[:, 0:16, :].reshape(FEEDS, 128)
    xi = r1_ref[:, 16:32, :].reshape(FEEDS, 128)
    x = jnp.concatenate([xr, xi], axis=1)
    re, im = [], []
    for c in range(4):
        g = mm(oh_ref[c * 256 : c * 256 + 256, :], x)
        re.append(g[:, :128])
        im.append(g[:, 128:])
    a_hi, a_lo = a_hi_ref[...], a_lo_ref[...]
    er, ei = re[0] + re[2], im[0] + im[2]
    fr, fi = re[1] + re[3], im[1] + im[3]
    dr, di = re[0] - re[2], im[0] - im[2]
    gr, gi = re[1] - re[3], im[1] - im[3]
    parts = [(er + fr, ei + fi), (dr + gi, di - gr), (er - fr, ei - fi), (dr - gi, di + gr)]
    for be in range(4):
        hr, hi = parts[be]
        top = jnp.concatenate([hr, hi], axis=1)
        low = jnp.concatenate([hi, -hr], axis=1)
        b_hi, b_lo = split(jnp.concatenate([top, low], axis=0))
        res = (mm(a_hi, b_hi) + (mm(a_hi, b_lo) + mm(a_lo, b_hi))).astype(BF16)
        b_ref[be * 8 : be * 8 + 8, 0] = res[:, :128].reshape(8, 32, 128)
        b_ref[be * 8 : be * 8 + 8, 1] = res[:, 128:].reshape(8, 32, 128)


def fill_spectrum(f_ref):
    def body(i, carry):
        row = lax.broadcasted_iota(jnp.int32, (128, 1024), 0) + i * 128
        lane = lax.broadcasted_iota(jnp.int32, (128, 1024), 1)
        w = (row >> 5) + 1
        steps = w * (lane >> 4) + ((row >> 4) & 1) * 16
        value = jnp.where((row & 15) == (lane & 15), cos_turns(steps, 64), 0.0)
        f_ref[pl.ds(pl.multiple_of(i * 128, 128), 128), :] = value.astype(BF16)
        return carry

    lax.fori_loop(0, 8, body, 0)


def fill_trials(delay_ref, tab_ref):
    dt = jnp.transpose(delay_ref[...].astype(F32)).astype(jnp.int32)
    dd = jnp.concatenate([dt, dt], axis=1)
    rows = []
    for rb in range(32):
        d = ((rb // 2) % 4) * 4 + rb // 8
        rows.append(dd[d * 8 : d * 8 + 8, :])
    step = jnp.concatenate(rows, axis=0)
    row = lax.broadcasted_iota(jnp.int32, (256, 128), 0)
    lane = lax.broadcasted_iota(jnp.int32, (256, 128), 1)
    start = 64 + 16 * (((row >> 3) & 1) - (lane >> 6))

    def body(q, phase):
        for k in range(4):
            phase = phase + step
            tab_ref[q, :, k * 128 : k * 128 + 128] = cos_turns(phase, 64).astype(BF16)
        return phase

    lax.fori_loop(0, 8, body, start)


def fill_inverse(m_ref):
    for w4 in range(4):
        row = lax.broadcasted_iota(jnp.int32, (128, 512), 0)
        lane = lax.broadcasted_iota(jnp.int32, (128, 512), 1)
        w = (row >> 4) * 4 + w4 + 1
        steps = w * (lane & 63) + ((row >> 3) & 1) * 16
        value = jnp.where((row & 7) == (lane >> 6), cos_turns(steps, 64), 0.0)
        scale = jnp.where(w == FRAMES // 2, 1.0, 2.0) * (1.0 / (FRAMES * math.sqrt(FINE)))
        m_ref[w4] = value * scale


def power(block, c_hi_ref, c_lo_ref, out_ref, cc_ref):
    c_hi, c_lo = c_hi_ref[...], c_lo_ref[...]
    zero = jnp.zeros((32, 128), BF16)
    for j in range(4):
        cur = [jnp.concatenate([block(j, t, r) for t in range(8)], axis=0) for r in range(2)]
        old = [jnp.concatenate([zero, cur[r][:224]], axis=0) for r in range(2)]
        left = jnp.concatenate(old + cur, axis=1)
        y = mm(left, c_hi) + mm(left, c_lo)
        p = y[:, :128] * y[:, :128] + y[:, 128:] * y[:, 128:]
        total = p[0:32]
        for t in range(1, 8):
            total = total + p[t * 32 : t * 32 + 32]
        for shift in (16, 32, 64):
            total = total + pltpu.roll(total, shift, 1)
        mean = total * (1.0 / FRAMES)
        for t in range(8):
            pt = p[t * 32 : t * 32 + 32]
            out_ref[pl.ds(t * 4 + j, 32, stride=32), :] = pt
            cc_ref[j * 32 : j * 32 + 32, t * 128 : t * 128 + 128] = (pt - mean).astype(BF16)


def dedisperse(f_ref, cc_ref, tab_ref, z_ref):
    cc = cc_ref[...]
    group = lax.broadcasted_iota(jnp.int32, (16, 128), 1) >> 5
    for q in range(8):
        s = lax.dot_general(
            f_ref[q * 128 : q * 128 + 128, :], cc, (((1,), (1,)), ((), ())), preferred_element_type=F32
        )
        turned = [s] + [pltpu.roll(s, 32 * k, 1) for k in range(1, 4)]
        rows = []
        for w4 in range(4):
            for r in range(2):
                for j in range(4):
                    at = (w4 * 2 + r) * 16
                    part = turned[(w4 - j) % 4][at : at + 16]
                    rows.append(jnp.where(group == w4, part, 0.0).astype(BF16))
        right = jnp.concatenate(rows, axis=0)
        z = mm(tab_ref[q], right).astype(BF16)
        z_ref[:, :, q * 128 : q * 128 + 128] = z.reshape(4, 64, 128)


def series(zs, m_ref, out_ref):
    v = jnp.concatenate([zs[:, q * 128 : q * 128 + 128] for q in range(8)], axis=0)
    vt = jnp.transpose(v)
    res = jnp.zeros((32, 512), F32)
    for w4 in range(4):
        res = res + jnp.dot(
            vt[w4 * 32 : w4 * 32 + 32], m_ref[w4], precision=lax.Precision.HIGHEST, preferred_element_type=F32
        )
    for d in range(8):
        out_ref[pl.ds(d, 32, stride=8), :] = res[:, d * 64 : d * 64 + 64]


def call(kernel, out, scratch=(), **kw):
    outs = out if isinstance(out, (list, tuple)) else [out]
    spec = pl.BlockSpec(memory_space=pltpu.VMEM)

    def run(*args):
        return pl.pallas_call(
            kernel,
            out_shape=out,
            in_specs=[spec] * len(args),
            out_specs=spec if not isinstance(out, (list, tuple)) else [spec] * len(outs),
            scratch_shapes=list(scratch),
            compiler_params=pltpu.CompilerParams(vmem_limit_bytes=60 << 20),
            **kw,
        )(*args)

    return run


def k_relayout(v_ref, s_ref):
    relayout(v_ref, s_ref)


def k_beam(pos_ref, r1_ref, ah_ref, al_ref, b_ref, oh_ref):
    fill_places(pos_ref, oh_ref)
    beamform(oh_ref, r1_ref, ah_ref, al_ref, b_ref)


def k_power(r2_ref, ch_ref, cl_ref, delay_ref, i_ref, z_ref, cc_ref, f_ref, tab_ref):
    fill_spectrum(f_ref)
    fill_trials(delay_ref, tab_ref)

    def block(j, t, r):
        return r2_ref[j, t % 2, t // 2, r]

    power(block, ch_ref, cl_ref, i_ref, cc_ref)
    dedisperse(f_ref, cc_ref, tab_ref, z_ref)


def k_series(z_ref, o_ref, m_ref):
    fill_inverse(m_ref)
    zs = z_ref[0].astype(F32)
    for k in range(1, 4):
        zs = zs + z_ref[k].astype(F32)
    series(zs, m_ref, o_ref)


def S(shape, dtype):
    return jax.ShapeDtypeStruct(shape, dtype)


run_relayout = call(k_relayout, S((128, 32, 128), BF16))
run_beam = call(k_beam, S((32, 2, 32, 128), BF16), [pltpu.VMEM((1024, FEEDS), BF16)])
run_power = call(
    k_power,
    [S((1024, 128), F32), S((4, 64, 1024), BF16)],
    [pltpu.VMEM((128, 1024), BF16), pltpu.VMEM((1024, 1024), BF16), pltpu.VMEM((8, 256, 512), BF16)],
)
run_series = call(k_series, S((256, 64), F32), [pltpu.VMEM((4, 128, 512), F32)])


def per_device(voltages, positions, delays):
    a_hi, a_lo = table_split(north_table())
    c_hi, c_lo = table_split(filter_table())
    s1 = run_relayout(voltages)
    r1 = lax.all_to_all(s1, ("z_hi", "x", "z_lo", "core"), 0, 0, tiled=True)
    pos = positions.reshape(8, 16, 16).swapaxes(0, 1).reshape(1, FEEDS)
    b = run_beam(pos, r1, a_hi, a_lo)
    r2 = lax.all_to_all(b, ("z_lo", "core", "tm"), 0, 0, tiled=True)
    i, z = run_power(r2.reshape(4, 2, 4, 2, 32, 128), c_hi, c_lo, delays.T)
    z = lax.all_to_all(z, "x", 0, 0, tiled=True)
    z = z.astype(F32).sum(axis=0).astype(BF16).reshape(4, 16, 1024)
    z = lax.all_to_all(z, "z_hi", 0, 0, tiled=True)
    d = run_series(z)
    i = i.reshape(32, 8, 4, 128).swapaxes(1, 2).reshape(32, 4, 1024)
    return i, d.reshape(32, 8, 64)


def solution(mesh):
    finer = Mesh(mesh.devices.reshape(4, 4, 4, 4, 2), ("z_hi", "x", "tm", "z_lo", "core"))
    beam, channel = ("z_lo", "core"), ("z_hi", "x")
    return jax.shard_map(
        per_device,
        mesh=finer,
        in_specs=(P(None, beam + channel, None, "tm"), P(), P(None, channel)),
        out_specs=(P(beam + ("tm",), channel, None), P(beam + ("tm",), channel, None)),
        check_vma=False,
    )
```

```python
import math

import jax
import jax.numpy as jnp
import numpy as np
from jax import lax
from jax.experimental import pallas as pl
from jax.experimental.pallas import tpu as pltpu
from jax.sharding import PartitionSpec as P

F32 = jnp.float32
BF16 = jnp.bfloat16
FEEDS = 2048
TAPS = 8
UPCH = 16
FRAMES = 64
FINE = 1024


def cos_turns(steps, period):
    left = (steps & (period - 1)) - period // 2
    u = jnp.abs(left).astype(F32) * (4.0 / period) - 1.0
    u2 = u * u
    p = -3.598843235e-06
    for c in (1.604411848e-04, -4.681754135e-03, 7.969262625e-02, -6.459640975e-01, 1.570796327e00):
        p = p * u2 + c
    return p * u


def split(value):
    high = value.astype(BF16)
    return high, (value - high.astype(F32)).astype(BF16)


def mm(a, b):
    return jnp.dot(a, b, preferred_element_type=F32)


def table_split(table):
    table = jnp.asarray(table.astype(np.float32))
    high = table.astype(BF16)
    return high, (table - high.astype(F32)).astype(BF16)


def north_table():
    n = np.arange(256)
    angle = 2 * np.pi * (n[:, None] * n[None, :] % 256) / 256
    return np.concatenate([np.cos(angle), np.sin(angle)], axis=1) / math.sqrt(FEEDS)


def filter_table():
    length = TAPS * UPCH
    j = np.arange(length)
    h = np.sinc((j - (length - 1) / 2) / UPCH) * (0.5 - 0.5 * np.cos(2 * np.pi * (j + 0.5) / length))
    h = h / np.sqrt(np.sum(h * h))
    s = np.arange(256)
    out = np.arange(128)
    tap = (s[:, None] // 16 - 8) - out[None, :] // 16 + 7
    m = s % 16
    used = (tap >= 0) & (tap < 8)
    weight = np.where(used, h[np.clip(tap, 0, 7) * 16 + m[:, None]], 0.0)
    angle = 2 * np.pi * (m[:, None] * (out % 16)[None, :] % 16) / 16
    c = (weight * np.cos(angle)).reshape(2, 128, 128)
    d = (weight * np.sin(angle)).reshape(2, 128, 128)
    real_in = np.concatenate([c, -d], axis=2)
    imag_in = np.concatenate([d, c], axis=2)
    return np.stack([real_in, imag_in], axis=1).reshape(512, 256)


def relayout(v_ref, s_ref):
    for g in range(8):
        for h in range(2):
            x = v_ref[:, :, g * 8 : g * 8 + 8, h * 128 : h * 128 + 128]
            x = x.astype(F32).reshape(32, 8, 128)
            y = jnp.swapaxes(x, 0, 1).astype(BF16)
            for c in range(8):
                s_ref[(g * 8 + c) * 2 + h] = y[c]


def fill_places(pos_ref, oh_ref):
    pos = pos_ref[...]

    def body(i, carry):
        row = lax.broadcasted_iota(jnp.int32, (128, FEEDS), 0) + i * 128
        hit = jnp.where(row == pos, 1.0, 0.0).astype(BF16)
        oh_ref[pl.ds(pl.multiple_of(i * 128, 128), 128), :] = hit
        return carry

    lax.fori_loop(0, 8, body, 0)


def grid_sums(oh_ref, r1_ref, hh_ref, hl_ref):
    xr = r1_ref[:, 0:16, :].reshape(FEEDS, 128)
    xi = r1_ref[:, 16:32, :].reshape(FEEDS, 128)
    x = jnp.concatenate([xr, xi], axis=1)
    re, im = [], []
    for c in range(4):
        g = mm(oh_ref[c * 256 : c * 256 + 256, :], x)
        re.append(g[:, :128])
        im.append(g[:, 128:])
    er, ei = re[0] + re[2], im[0] + im[2]
    fr, fi = re[1] + re[3], im[1] + im[3]
    dr, di = re[0] - re[2], im[0] - im[2]
    gr, gi = re[1] - re[3], im[1] - im[3]
    parts = [(er + fr, ei + fi), (dr + gi, di - gr), (er - fr, ei - fi), (dr - gi, di + gr)]
    for be in range(4):
        hr, hi = parts[be]
        top = jnp.concatenate([hr, hi], axis=1)
        low = jnp.concatenate([hi, -hr], axis=1)
        hh_ref[be], hl_ref[be] = split(jnp.concatenate([top, low], axis=0))


def north_beams(be, hh_ref, hl_ref, a_hi, a_lo, b_ref):
    b_hi, b_lo = hh_ref[be], hl_ref[be]
    res = (mm(a_hi, b_hi) + (mm(a_hi, b_lo) + mm(a_lo, b_hi))).astype(BF16)
    b_ref[pl.ds(be * 8, 8), 0] = res[:, :128].reshape(8, 32, 128)
    b_ref[pl.ds(be * 8, 8), 1] = res[:, 128:].reshape(8, 32, 128)


def fill_spectrum(f_ref):
    def body(i, carry):
        row = lax.broadcasted_iota(jnp.int32, (128, 1024), 0) + i * 128
        lane = lax.broadcasted_iota(jnp.int32, (128, 1024), 1)
        w = (row >> 5) + 1
        steps = w * (lane >> 4) + ((row >> 4) & 1) * 16
        value = jnp.where((row & 15) == (lane & 15), cos_turns(steps, 64), 0.0)
        f_ref[pl.ds(pl.multiple_of(i * 128, 128), 128), :] = value.astype(BF16)
        return carry

    lax.fori_loop(0, 8, body, 0)


def fill_trials(delay_ref, tab_ref):
    dt = jnp.transpose(delay_ref[...].astype(F32)).astype(jnp.int32)
    dd = jnp.concatenate([dt, dt], axis=1)
    rows = []
    for rb in range(32):
        d = ((rb // 2) % 4) * 4 + rb // 8
        rows.append(dd[d * 8 : d * 8 + 8, :])
    step = jnp.concatenate(rows, axis=0)
    row = lax.broadcasted_iota(jnp.int32, (256, 128), 0)
    lane = lax.broadcasted_iota(jnp.int32, (256, 128), 1)
    start = 64 + 16 * (((row >> 3) & 1) - (lane >> 6))

    def body(q, phase):
        for k in range(4):
            phase = phase + step
            tab_ref[q, :, k * 128 : k * 128 + 128] = cos_turns(phase, 64).astype(BF16)
        return phase

    lax.fori_loop(0, 8, body, start)


def fill_inverse(m_ref):
    for w4 in range(4):
        row = lax.broadcasted_iota(jnp.int32, (128, 512), 0)
        lane = lax.broadcasted_iota(jnp.int32, (128, 512), 1)
        w = (row >> 4) * 4 + w4 + 1
        steps = w * (lane & 63) + ((row >> 3) & 1) * 16
        value = jnp.where((row & 7) == (lane >> 6), cos_turns(steps, 64), 0.0)
        scale = jnp.where(w == FRAMES // 2, 1.0, 2.0) * (1.0 / (FRAMES * math.sqrt(FINE)))
        m_ref[w4] = value * scale


def power(block, c_hi_ref, c_lo_ref, out_ref, cc_ref):
    c_hi, c_lo = c_hi_ref[...], c_lo_ref[...]
    zero = jnp.zeros((32, 128), BF16)
    for j in range(4):
        cur = [jnp.concatenate([block(j, t, r) for t in range(8)], axis=0) for r in range(2)]
        old = [jnp.concatenate([zero, cur[r][:224]], axis=0) for r in range(2)]
        left = jnp.concatenate(old + cur, axis=1)
        y = mm(left, c_hi) + mm(left, c_lo)
        p = y[:, :128] * y[:, :128] + y[:, 128:] * y[:, 128:]
        total = p[0:32]
        for t in range(1, 8):
            total = total + p[t * 32 : t * 32 + 32]
        for shift in (16, 32, 64):
            total = total + pltpu.roll(total, shift, 1)
        mean = total * (1.0 / FRAMES)
        for t in range(8):
            pt = p[t * 32 : t * 32 + 32]
            out_ref[pl.ds(t * 4 + j, 32, stride=32), :] = pt
            cc_ref[j * 32 : j * 32 + 32, t * 128 : t * 128 + 128] = (pt - mean).astype(BF16)


def bin_quad(q, f_ref, cc_ref, tab_ref):
    group = lax.broadcasted_iota(jnp.int32, (16, 128), 1) >> 5
    s = lax.dot_general(
        f_ref[q * 128 : q * 128 + 128, :], cc_ref[...], (((1,), (1,)), ((), ())), preferred_element_type=F32
    )
    turned = [s] + [pltpu.roll(s, 32 * k, 1) for k in range(1, 4)]
    rows = []
    for w4 in range(4):
        for r in range(2):
            for j in range(4):
                at = (w4 * 2 + r) * 16
                part = turned[(w4 - j) % 4][at : at + 16]
                rows.append(jnp.where(group == w4, part, 0.0).astype(BF16))
    right = jnp.concatenate(rows, axis=0)
    return mm(tab_ref[q], right).astype(BF16).reshape(4, 64, 128)


def series(v, m_ref, out_ref):
    vt = jnp.transpose(v)
    res = jnp.zeros((32, 512), F32)
    for w4 in range(4):
        res = res + jnp.dot(
            vt[w4 * 32 : w4 * 32 + 32], m_ref[w4], precision=lax.Precision.HIGHEST, preferred_element_type=F32
        )
    for d in range(8):
        out_ref[pl.ds(d, 32, stride=8), :] = res[:, d * 64 : d * 64 + 64]


MESH = pl.DeviceIdType.MESH


def kernel(
    v_ref, pos_ref, delay_ref, ah_any, al_any, ch_any, cl_any,
    i_ref, d_ref,
    vbuf, ah, al, ch, cl, s1, r1, oh, hh, hl, b, r2, cc, f, tab, m, z, rx, zz, rz,
    load, send1, recv1, send2, recv2, sendx, recvx, sendz, recvz,
):
    channel, tm, beam = lax.axis_index("channel"), lax.axis_index("tm"), lax.axis_index("beam")
    z_hi, x, z_lo, core = channel >> 2, channel & 3, beam >> 1, beam & 1
    place = z_hi * 4 + z_lo

    loads = [
        pltpu.make_async_copy(src, dst, load.at[n])
        for n, (src, dst) in enumerate([(v_ref, vbuf), (ah_any, ah), (al_any, al), (ch_any, ch), (cl_any, cl)])
    ]
    for copy in loads:
        copy.start()

    def plane(act):
        def around(to, dx, dc):
            act(((to >> 2) << 2) + ((x + dx) & 3), ((to & 3) << 1) + ((core + dc) & 1))

        def step(n, carry):
            left = 15 - n
            far = ((left + 1) >> 1) * (((left & 1) << 1) - 1)
            to = (place + far + 16) & 15
            for dx in range(4):
                for dc in range(2):
                    around(to, dx, dc)
            return carry

        lax.fori_loop(0, 15, step, 0)
        for dx in range(4):
            for dc in range(2):
                if dx or dc:
                    around(place, dx, dc)

    barrier = pltpu.get_barrier_semaphore()

    def greet(c, bm):
        pl.semaphore_signal(barrier, inc=1, device_id={"channel": c, "tm": tm, "beam": bm}, device_id_type=MESH)

    plane(greet)
    for n in range(1, 4):
        for bm in range(8):
            pl.semaphore_signal(
                barrier, inc=1, device_id={"channel": channel, "tm": (tm + n) & 3, "beam": bm}, device_id_type=MESH
            )
    loads[0].wait()
    relayout(vbuf, s1)
    fill_places(pos_ref, oh)
    pl.semaphore_wait(barrier, 151)

    def remote(src, dst, send, recv, c, t, bm):
        return pltpu.make_async_remote_copy(
            src_ref=src, dst_ref=dst, send_sem=send, recv_sem=recv,
            device_id={"channel": c, "tm": t, "beam": bm}, device_id_type=MESH,
        )

    def bulk(src, dst, send, recv):
        return remote(src, dst, send, recv, channel, tm, beam ^ 1)

    feed = beam * 16 + channel
    plane(lambda c, bm: remote(s1.at[c * 8 + bm], r1.at[feed], send1, recv1, c, tm, bm).start())
    r1[feed] = s1[channel * 8 + beam]
    fill_spectrum(f)
    fill_trials(delay_ref, tab)
    fill_inverse(m)
    for copy in loads[1:]:
        copy.wait()
    first = bulk(s1.at[pl.ds(0, 127)], r1.at[pl.ds(0, 127)], send1, recv1)
    first.wait_recv()

    grid_sums(oh, r1, hh, hl)
    slot = z_lo * 8 + tm * 2 + core
    a_hi, a_lo = ah[...], al[...]

    def pass_on(be, own):
        for dc in range(2):
            for dt in range(4):
                if own and dc == 0 and dt == 0:
                    continue
                co, t = (core + dc) & 1, (tm + dt) & 3
                remote(b.at[be * 8 + co * 4 + t], r2.at[slot], send2, recv2, channel, t, be * 2 + co).start()

    east = [(z_lo + 3 - n) & 3 for n in range(4)]
    for n in range(4):
        north_beams(east[n], hh, hl, a_hi, a_lo, b)
        if n:
            pass_on(east[n - 1], False)
    r2[slot] = b[z_lo * 8 + core * 4 + tm]
    pass_on(z_lo, True)
    second = bulk(b.at[pl.ds(0, 31)], r2.at[pl.ds(0, 31)], send2, recv2)
    second.wait_recv()

    power(lambda j, t, r: r2[j * 8 + t, r], ch, cl, i_ref, cc)

    def to_x(q):
        for n in range(1, 4):
            to = (x + n) & 3
            remote(z.at[q, to], rx.at[x, q], sendx.at[q // 4], recvx.at[q // 4], z_hi * 4 + to, tm, beam).start()

    for q in range(8):
        z[q] = bin_quad(q, f, cc, tab)
        if q:
            to_x(q - 1)
            rx[x, q - 1] = z[q - 1, x]
    rx[x, 7] = z[7, x]
    to_x(7)

    def to_z(half):
        quads = pl.ds(half * 4, 4)
        for n in range(1, 4):
            to = (z_hi + n) & 3
            remote(
                zz.at[to, quads], rz.at[z_hi, quads], sendz.at[half], recvz.at[half], to * 4 + x, tm, beam
            ).start()

    def sums_x(half):
        for q in range(half * 4, half * 4 + 4):
            total = rx[0, q].astype(F32)
            for n in range(1, 4):
                total = total + rx[n, q].astype(F32)
            zz[:, q] = total.astype(BF16).reshape(4, 16, 128)

    x_copies = [bulk(rx.at[pl.ds(0, 3), pl.ds(0, 4)], rx.at[pl.ds(0, 3), pl.ds(0, 4)], sendx.at[n], recvx.at[n]) for n in range(2)]
    z_copies = [bulk(zz.at[pl.ds(0, 3), pl.ds(0, 4)], rz.at[pl.ds(0, 3), pl.ds(0, 4)], sendz.at[n], recvz.at[n]) for n in range(2)]
    for half in range(2):
        x_copies[half].wait_recv()
        sums_x(half)
        rz[z_hi, pl.ds(half * 4, 4)] = zz[z_hi, pl.ds(half * 4, 4)]
        to_z(half)
    first.wait_send()
    second.wait_send()
    for half in range(2):
        x_copies[half].wait_send()
    for half in range(2):
        z_copies[half].wait_recv()
    total = rz[0].astype(F32)
    for n in range(1, 4):
        total = total + rz[n].astype(F32)
    series(total.reshape(128, 128), m, d_ref)
    for half in range(2):
        z_copies[half].wait_send()


def S(shape, dtype):
    return jax.ShapeDtypeStruct(shape, dtype)


def per_device(voltages, positions, delays):
    tables = table_split(north_table()) + table_split(filter_table())
    vmem = pl.BlockSpec(memory_space=pltpu.VMEM)
    hbm = pl.BlockSpec(memory_space=pl.ANY)
    V = pltpu.VMEM
    dma = pltpu.SemaphoreType.DMA
    i, d = pl.pallas_call(
        kernel,
        out_shape=[S((1024, 128), F32), S((256, 64), F32)],
        in_specs=[hbm, vmem, vmem] + [hbm] * 4,
        out_specs=[vmem, vmem],
        scratch_shapes=[
            V((2, 16, 64, 256), BF16),
            V((256, 512), BF16),
            V((256, 512), BF16),
            V((512, 256), BF16),
            V((512, 256), BF16),
            V((128, 32, 128), BF16),
            V((128, 32, 128), BF16),
            V((1024, FEEDS), BF16),
            V((4, 512, 256), BF16),
            V((4, 512, 256), BF16),
            V((32, 2, 32, 128), BF16),
            V((32, 2, 32, 128), BF16),
            V((128, 1024), BF16),
            V((1024, 1024), BF16),
            V((8, 256, 512), BF16),
            V((4, 128, 512), F32),
            V((8, 4, 64, 128), BF16),
            V((4, 8, 64, 128), BF16),
            V((4, 8, 16, 128), BF16),
            V((4, 8, 16, 128), BF16),
            dma((5,)),
            dma,
            dma,
            dma,
            dma,
            dma((2,)),
            dma((2,)),
            dma((2,)),
            dma((2,)),
        ],
        compiler_params=pltpu.CompilerParams(collective_id=0, has_side_effects=True, vmem_limit_bytes=60 << 20),
    )(voltages, positions.reshape(1, FEEDS), delays.T, *tables)
    i = i.reshape(32, 8, 4, 128).swapaxes(1, 2).reshape(32, 4, 1024)
    return i, d.reshape(32, 8, 64)


def solution(mesh):
    beam = ("beam", "tm")
    return jax.shard_map(
        per_device,
        mesh=mesh,
        in_specs=(P(None, ("beam", "channel"), None, "tm"), P(), P(None, "channel")),
        out_specs=(P(beam, "channel", None), P(beam, "channel", None)),
        check_vma=False,
    )
```

```python
import math

import jax
import jax.numpy as jnp
import numpy as np
from jax import lax
from jax.experimental import pallas as pl
from jax.experimental.pallas import tpu as pltpu
from jax.sharding import PartitionSpec as P

F32 = jnp.float32
BF16 = jnp.bfloat16
FEEDS = 2048
TAPS = 8
UPCH = 16
FRAMES = 64
FINE = 1024
PIECES = 4
QUADS = 8 // PIECES


def cos_turns(steps, period):
    left = (steps & (period - 1)) - period // 2
    u = jnp.abs(left).astype(F32) * (4.0 / period) - 1.0
    u2 = u * u
    p = -3.598843235e-06
    for c in (1.604411848e-04, -4.681754135e-03, 7.969262625e-02, -6.459640975e-01, 1.570796327e00):
        p = p * u2 + c
    return p * u


def split(value):
    high = value.astype(BF16)
    return high, (value - high.astype(F32)).astype(BF16)


def mm(a, b):
    return jnp.dot(a, b, preferred_element_type=F32)


def table_split(table):
    table = jnp.asarray(table.astype(np.float32))
    high = table.astype(BF16)
    return high, (table - high.astype(F32)).astype(BF16)


def north_table():
    n = np.arange(256)
    angle = 2 * np.pi * (n[:, None] * n[None, :] % 256) / 256
    return np.concatenate([np.cos(angle), np.sin(angle)], axis=1) / math.sqrt(FEEDS)


def filter_table():
    length = TAPS * UPCH
    j = np.arange(length)
    h = np.sinc((j - (length - 1) / 2) / UPCH) * (0.5 - 0.5 * np.cos(2 * np.pi * (j + 0.5) / length))
    h = h / np.sqrt(np.sum(h * h))
    s = np.arange(256)
    out = np.arange(128)
    tap = (s[:, None] // 16 - 8) - out[None, :] // 16 + 7
    m = s % 16
    used = (tap >= 0) & (tap < 8)
    weight = np.where(used, h[np.clip(tap, 0, 7) * 16 + m[:, None]], 0.0)
    angle = 2 * np.pi * (m[:, None] * (out % 16)[None, :] % 16) / 16
    c = (weight * np.cos(angle)).reshape(2, 128, 128)
    d = (weight * np.sin(angle)).reshape(2, 128, 128)
    real_in = np.concatenate([c, -d], axis=2)
    imag_in = np.concatenate([d, c], axis=2)
    return np.stack([real_in, imag_in], axis=1).reshape(512, 256)


def relayout(v_ref, s_ref):
    for g in range(8):
        for h in range(2):
            x = v_ref[:, :, g * 8 : g * 8 + 8, h * 128 : h * 128 + 128]
            x = x.astype(F32).reshape(32, 8, 128)
            y = jnp.swapaxes(x, 0, 1).astype(BF16)
            for c in range(8):
                s_ref[(g * 8 + c) * 2 + h] = y[c]


def fill_places(pos_ref, oh_ref):
    pos = pos_ref[...]

    def body(i, carry):
        row = lax.broadcasted_iota(jnp.int32, (128, FEEDS), 0) + i * 128
        hit = jnp.where(row == pos, 1.0, 0.0).astype(BF16)
        oh_ref[pl.ds(pl.multiple_of(i * 128, 128), 128), :] = hit
        return carry

    lax.fori_loop(0, 8, body, 0)


def grid_sums(oh_ref, r1_ref, hh_ref, hl_ref):
    xr = r1_ref[:, 0:16, :].reshape(FEEDS, 128)
    xi = r1_ref[:, 16:32, :].reshape(FEEDS, 128)
    x = jnp.concatenate([xr, xi], axis=1)
    re, im = [], []
    for c in range(4):
        g = mm(oh_ref[c * 256 : c * 256 + 256, :], x)
        re.append(g[:, :128])
        im.append(g[:, 128:])
    er, ei = re[0] + re[2], im[0] + im[2]
    fr, fi = re[1] + re[3], im[1] + im[3]
    dr, di = re[0] - re[2], im[0] - im[2]
    gr, gi = re[1] - re[3], im[1] - im[3]
    parts = [(er + fr, ei + fi), (dr + gi, di - gr), (er - fr, ei - fi), (dr - gi, di + gr)]
    for be in range(4):
        hr, hi = parts[be]
        top = jnp.concatenate([hr, hi], axis=1)
        low = jnp.concatenate([hi, -hr], axis=1)
        hh_ref[be], hl_ref[be] = split(jnp.concatenate([top, low], axis=0))


def north_beams(be, hh_ref, hl_ref, a_hi, a_lo, b_ref):
    b_hi, b_lo = hh_ref[be], hl_ref[be]
    res = (mm(a_hi, b_hi) + (mm(a_hi, b_lo) + mm(a_lo, b_hi))).astype(BF16)
    b_ref[pl.ds(be * 8, 8), 0] = res[:, :128].reshape(8, 32, 128)
    b_ref[pl.ds(be * 8, 8), 1] = res[:, 128:].reshape(8, 32, 128)


def fill_spectrum(f_ref):
    def body(i, carry):
        row = lax.broadcasted_iota(jnp.int32, (128, 1024), 0) + i * 128
        lane = lax.broadcasted_iota(jnp.int32, (128, 1024), 1)
        w = (row >> 5) + 1
        steps = w * (lane >> 4) + ((row >> 4) & 1) * 16
        value = jnp.where((row & 15) == (lane & 15), cos_turns(steps, 64), 0.0)
        f_ref[pl.ds(pl.multiple_of(i * 128, 128), 128), :] = value.astype(BF16)
        return carry

    lax.fori_loop(0, 8, body, 0)


def fill_trials(delay_ref, tab_ref):
    dt = jnp.transpose(delay_ref[...].astype(F32)).astype(jnp.int32)
    dd = jnp.concatenate([dt, dt], axis=1)
    rows = []
    for rb in range(32):
        d = ((rb // 2) % 4) * 4 + rb // 8
        rows.append(dd[d * 8 : d * 8 + 8, :])
    step = jnp.concatenate(rows, axis=0)
    row = lax.broadcasted_iota(jnp.int32, (256, 128), 0)
    lane = lax.broadcasted_iota(jnp.int32, (256, 128), 1)
    start = 64 + 16 * (((row >> 3) & 1) - (lane >> 6))

    def body(q, phase):
        for k in range(4):
            phase = phase + step
            tab_ref[q, :, k * 128 : k * 128 + 128] = cos_turns(phase, 64).astype(BF16)
        return phase

    lax.fori_loop(0, 8, body, start)


def fill_inverse(mh_ref, ml_ref):
    for w4 in range(4):
        row = lax.broadcasted_iota(jnp.int32, (128, 512), 0)
        lane = lax.broadcasted_iota(jnp.int32, (128, 512), 1)
        w = (row >> 4) * 4 + w4 + 1
        steps = w * (lane & 63) + ((row >> 3) & 1) * 16
        value = jnp.where((row & 7) == (lane >> 6), cos_turns(steps, 64), 0.0)
        scale = jnp.where(w == FRAMES // 2, 1.0, 2.0) * (1.0 / (FRAMES * math.sqrt(FINE)))
        mh_ref[w4], ml_ref[w4] = split(value * scale)


def power(block, c_hi_ref, c_lo_ref, out_ref, cc_ref):
    c_hi, c_lo = c_hi_ref[...], c_lo_ref[...]
    zero = jnp.zeros((32, 128), BF16)
    for j in range(4):
        cur = [jnp.concatenate([block(j, t, r) for t in range(8)], axis=0) for r in range(2)]
        old = [jnp.concatenate([zero, cur[r][:224]], axis=0) for r in range(2)]
        left = jnp.concatenate(old + cur, axis=1)
        y = mm(left, c_hi) + mm(left, c_lo)
        p = y[:, :128] * y[:, :128] + y[:, 128:] * y[:, 128:]
        total = p[0:32]
        for t in range(1, 8):
            total = total + p[t * 32 : t * 32 + 32]
        for shift in (16, 32, 64):
            total = total + pltpu.roll(total, shift, 1)
        mean = total * (1.0 / FRAMES)
        for t in range(8):
            pt = p[t * 32 : t * 32 + 32]
            out_ref[pl.ds(t * 4 + j, 32, stride=32), :] = pt
            cc_ref[j * 32 : j * 32 + 32, t * 128 : t * 128 + 128] = (pt - mean).astype(BF16)


def bin_quad(q, f_ref, cc_ref, tab_ref):
    group = lax.broadcasted_iota(jnp.int32, (16, 128), 1) >> 5
    s = lax.dot_general(
        f_ref[q * 128 : q * 128 + 128, :], cc_ref[...], (((1,), (1,)), ((), ())), preferred_element_type=F32
    )
    turned = [s] + [pltpu.roll(s, 32 * k, 1) for k in range(1, 4)]
    rows = []
    for w4 in range(4):
        for r in range(2):
            for j in range(4):
                at = (w4 * 2 + r) * 16
                part = turned[(w4 - j) % 4][at : at + 16]
                rows.append(jnp.where(group == w4, part, 0.0).astype(BF16))
    right = jnp.concatenate(rows, axis=0)
    return mm(tab_ref[q], right).astype(BF16).reshape(4, 64, 128)


def series(v, mh_ref, ml_ref, out_ref):
    v_hi, v_lo = split(jnp.transpose(v))
    res = jnp.zeros((32, 512), F32)
    for w4 in range(4):
        rows = slice(w4 * 32, w4 * 32 + 32)
        res = res + mm(v_hi[rows], mh_ref[w4]) + (mm(v_lo[rows], mh_ref[w4]) + mm(v_hi[rows], ml_ref[w4]))
    for d in range(8):
        out_ref[pl.ds(d, 32, stride=8), :] = res[:, d * 64 : d * 64 + 64]


MESH = pl.DeviceIdType.MESH


def kernel(
    v_ref, pos_ref, delay_ref, ah_any, al_any, ch_any, cl_any,
    i_out, d_ref,
    i_ref, vbuf, ah, al, ch, cl, s1, r1, oh, hh, hl, b, r2, cc, f, tab, mh, ml, z, rx, zz, rz,
    load, send1, recv1, send2, recv2, sendx, recvx, sendz, recvz, wave,
):
    channel, tm, beam = lax.axis_index("channel"), lax.axis_index("tm"), lax.axis_index("beam")
    z_hi, x, z_lo, core = channel >> 2, channel & 3, beam >> 1, beam & 1
    place = z_hi * 4 + z_lo

    loads = [
        pltpu.make_async_copy(src, dst, load.at[n])
        for n, (src, dst) in enumerate([(v_ref, vbuf), (ah_any, ah), (al_any, al), (ch_any, ch), (cl_any, cl)])
    ]
    for copy in loads:
        copy.start()

    def around(to, act):
        for dx in range(4):
            for dc in range(2):
                act(((to >> 2) << 2) + ((x + dx) & 3), ((to & 3) << 1) + ((core + dc) & 1))

    def rings(first, count, act):
        def step(n, carry):
            left = first - n
            far = ((left + 1) >> 1) * (((left & 1) << 1) - 1)
            around((place + far + 16) & 15, act)
            return carry

        lax.fori_loop(0, count, step, 0)

    def here(act):
        for dx in range(4):
            for dc in range(2):
                if dx or dc:
                    act((z_hi << 2) + ((x + dx) & 3), (z_lo << 1) + ((core + dc) & 1))

    barrier = pltpu.get_barrier_semaphore()

    def greet(c, bm):
        pl.semaphore_signal(barrier, inc=1, device_id={"channel": c, "tm": tm, "beam": bm}, device_id_type=MESH)

    rings(8, 8, greet)
    for n in range(1, 4):
        for bm in range(8):
            pl.semaphore_signal(
                barrier, inc=1, device_id={"channel": channel, "tm": (tm + n) & 3, "beam": bm}, device_id_type=MESH
            )
    here(greet)
    loads[0].wait()
    relayout(vbuf, s1)
    pl.semaphore_wait(barrier, 95)
    for n, turn in ((0, 1), (1, 3)):
        to = ((z_hi + turn) & 3) * 4 + x
        pl.semaphore_signal(
            wave.at[n], inc=1, device_id={"channel": to, "tm": tm, "beam": beam}, device_id_type=MESH
        )

    def remote(src, dst, send, recv, c, t, bm):
        return pltpu.make_async_remote_copy(
            src_ref=src, dst_ref=dst, send_sem=send, recv_sem=recv,
            device_id={"channel": c, "tm": t, "beam": bm}, device_id_type=MESH,
        )

    def bulk(src, dst, send, recv):
        return remote(src, dst, send, recv, channel, tm, beam ^ 1)

    feed = beam * 16 + channel

    def hand(c, bm):
        remote(s1.at[c * 8 + bm], r1.at[feed], send1, recv1, c, tm, bm).start()

    rings(6, 2, hand)
    pl.semaphore_wait(wave.at[0], 1)
    pl.semaphore_wait(wave.at[1], 1)
    rings(15, 9, hand)
    rings(4, 4, hand)
    here(hand)
    r1[feed] = s1[channel * 8 + beam]
    fill_places(pos_ref, oh)
    fill_spectrum(f)
    fill_trials(delay_ref, tab)
    fill_inverse(mh, ml)
    for copy in loads[1:]:
        copy.wait()
    first = bulk(s1.at[pl.ds(0, 127)], r1.at[pl.ds(0, 127)], send1, recv1)
    first.wait_recv()

    grid_sums(oh, r1, hh, hl)
    slot = z_lo * 8 + tm * 2 + core
    a_hi, a_lo = ah[...], al[...]

    def pass_on(be, own):
        for dc in range(2):
            for dt in range(4):
                if own and dc == 0 and dt == 0:
                    continue
                co, t = (core + dc) & 1, (tm + dt) & 3
                remote(b.at[be * 8 + co * 4 + t], r2.at[slot], send2, recv2, channel, t, be * 2 + co).start()

    east = [(z_lo + 3 - n) & 3 for n in range(4)]
    for n in range(4):
        north_beams(east[n], hh, hl, a_hi, a_lo, b)
        if n:
            pass_on(east[n - 1], False)
    r2[slot] = b[z_lo * 8 + core * 4 + tm]
    pass_on(z_lo, True)
    second = bulk(b.at[pl.ds(0, 31)], r2.at[pl.ds(0, 31)], send2, recv2)
    second.wait_recv()

    power(lambda j, t, r: r2[j * 8 + t, r], ch, cl, i_ref, cc)

    kept = pltpu.make_async_copy(i_ref, i_out, load.at[5])
    kept.start()

    def to_x(q):
        for n in range(1, 4):
            to = (x + n) & 3
            remote(z.at[q, to], rx.at[x, q], sendx.at[q // QUADS], recvx.at[q // QUADS], z_hi * 4 + to, tm, beam).start()

    for q in range(8):
        z[q] = bin_quad(q, f, cc, tab)
        if q:
            to_x(q - 1)
            rx[x, q - 1] = z[q - 1, x]
    rx[x, 7] = z[7, x]
    to_x(7)

    def to_z(piece):
        quads = pl.ds(piece * QUADS, QUADS)
        for n in range(1, 4):
            to = (z_hi + n) & 3
            remote(
                zz.at[to, quads], rz.at[z_hi, quads], sendz.at[piece], recvz.at[piece], to * 4 + x, tm, beam
            ).start()

    def sums_x(piece):
        for q in range(piece * QUADS, piece * QUADS + QUADS):
            total = rx[0, q].astype(F32)
            for n in range(1, 4):
                total = total + rx[n, q].astype(F32)
            zz[:, q] = total.astype(BF16).reshape(4, 16, 128)

    x_copies = [bulk(rx.at[pl.ds(0, 3), pl.ds(0, QUADS)], rx.at[pl.ds(0, 3), pl.ds(0, QUADS)], sendx.at[n], recvx.at[n]) for n in range(PIECES)]
    z_copies = [bulk(zz.at[pl.ds(0, 3), pl.ds(0, QUADS)], rz.at[pl.ds(0, 3), pl.ds(0, QUADS)], sendz.at[n], recvz.at[n]) for n in range(PIECES)]
    for piece in range(PIECES):
        x_copies[piece].wait_recv()
        sums_x(piece)
        rz[z_hi, pl.ds(piece * QUADS, QUADS)] = zz[z_hi, pl.ds(piece * QUADS, QUADS)]
        to_z(piece)
    kept.wait()
    first.wait_send()
    second.wait_send()
    for piece in range(PIECES):
        x_copies[piece].wait_send()
    for piece in range(PIECES):
        z_copies[piece].wait_recv()
    total = rz[0].astype(F32)
    for n in range(1, 4):
        total = total + rz[n].astype(F32)
    series(total.reshape(128, 128), mh, ml, d_ref)
    for piece in range(PIECES):
        z_copies[piece].wait_send()


def S(shape, dtype):
    return jax.ShapeDtypeStruct(shape, dtype)


def put_out(i_ref, d_ref, i_out, d_out, i_buf, d_buf, sems):
    pairs = [(i_ref.at[pl.ds(n * 256, 256)], i_buf.at[pl.ds(n * 256, 256)], i_out.at[pl.ds(n * 256, 256)]) for n in range(4)]
    pairs.append((d_ref, d_buf, d_out))
    come = [pltpu.make_async_copy(a, b, sems.at[0, n]) for n, (a, b, c) in enumerate(pairs)]
    go = [pltpu.make_async_copy(b, c, sems.at[1, n]) for n, (a, b, c) in enumerate(pairs)]
    for copy in come:
        copy.start()
    for n in range(5):
        come[n].wait()
        go[n].start()
    for copy in go:
        copy.wait()


def per_device(voltages, positions, delays):
    tables = table_split(north_table()) + table_split(filter_table())
    vmem = pl.BlockSpec(memory_space=pltpu.VMEM)
    hbm = pl.BlockSpec(memory_space=pl.ANY)
    V = pltpu.VMEM
    dma = pltpu.SemaphoreType.DMA
    i, d = pl.pallas_call(
        kernel,
        out_shape=[S((1024, 128), F32), S((256, 64), F32)],
        in_specs=[hbm, vmem, vmem] + [hbm] * 4,
        out_specs=[hbm, vmem],
        scratch_shapes=[
            V((1024, 128), F32),
            V((2, 16, 64, 256), BF16),
            V((256, 512), BF16),
            V((256, 512), BF16),
            V((512, 256), BF16),
            V((512, 256), BF16),
            V((128, 32, 128), BF16),
            V((128, 32, 128), BF16),
            V((1024, FEEDS), BF16),
            V((4, 512, 256), BF16),
            V((4, 512, 256), BF16),
            V((32, 2, 32, 128), BF16),
            V((32, 2, 32, 128), BF16),
            V((128, 1024), BF16),
            V((1024, 1024), BF16),
            V((8, 256, 512), BF16),
            V((4, 128, 512), BF16),
            V((4, 128, 512), BF16),
            V((8, 4, 64, 128), BF16),
            V((4, 8, 64, 128), BF16),
            V((4, 8, 16, 128), BF16),
            V((4, 8, 16, 128), BF16),
            dma((6,)),
            dma,
            dma,
            dma,
            dma,
            dma((PIECES,)),
            dma((PIECES,)),
            dma((PIECES,)),
            dma((PIECES,)),
            pltpu.SemaphoreType.REGULAR((2,)),
        ],
        compiler_params=pltpu.CompilerParams(collective_id=0, has_side_effects=True, vmem_limit_bytes=60 << 20),
    )(voltages, positions.reshape(1, FEEDS), delays.T, *tables)
    i, d = pl.pallas_call(
        put_out,
        out_shape=[S((1024, 128), F32), S((256, 64), F32)],
        in_specs=[hbm, hbm],
        out_specs=[hbm, hbm],
        scratch_shapes=[V((1024, 128), F32), V((256, 64), F32), dma((2, 5))],
    )(i, d)
    i = i.reshape(32, 8, 4, 128).swapaxes(1, 2).reshape(32, 4, 1024)
    return i, d.reshape(32, 8, 64)


def solution(mesh):
    beam = ("beam", "tm")
    return jax.shard_map(
        per_device,
        mesh=mesh,
        in_specs=(P(None, ("beam", "channel"), None, "tm"), P(), P(None, "channel")),
        out_specs=(P(beam, "channel", None), P(beam, "channel", None)),
        check_vma=False,
    )
```

```python
import math

import jax
import jax.numpy as jnp
import numpy as np
from jax import lax
from jax.experimental import pallas as pl
from jax.experimental.pallas import tpu as pltpu
from jax.sharding import PartitionSpec as P

F32 = jnp.float32
BF16 = jnp.bfloat16
FEEDS = 2048
TAPS = 8
UPCH = 16
FRAMES = 64
FINE = 1024


def cos_turns(steps, period):
    left = (steps & (period - 1)) - period // 2
    u = jnp.abs(left).astype(F32) * (4.0 / period) - 1.0
    u2 = u * u
    p = -3.598843235e-06
    for c in (1.604411848e-04, -4.681754135e-03, 7.969262625e-02, -6.459640975e-01, 1.570796327e00):
        p = p * u2 + c
    return p * u


def split(value):
    high = value.astype(BF16)
    return high, (value - high.astype(F32)).astype(BF16)


def mm(a, b):
    return jnp.dot(a, b, preferred_element_type=F32)


def table_split(table):
    table = jnp.asarray(table.astype(np.float32))
    high = table.astype(BF16)
    return high, (table - high.astype(F32)).astype(BF16)


def north_table():
    n = np.arange(256)
    angle = 2 * np.pi * (n[:, None] * n[None, :] % 256) / 256
    return np.concatenate([np.cos(angle), np.sin(angle)], axis=1) / math.sqrt(FEEDS)


def filter_table():
    length = TAPS * UPCH
    j = np.arange(length)
    h = np.sinc((j - (length - 1) / 2) / UPCH) * (0.5 - 0.5 * np.cos(2 * np.pi * (j + 0.5) / length))
    h = h / np.sqrt(np.sum(h * h))
    s = np.arange(256)
    out = np.arange(128)
    tap = (s[:, None] // 16 - 8) - out[None, :] // 16 + 7
    m = s % 16
    used = (tap >= 0) & (tap < 8)
    weight = np.where(used, h[np.clip(tap, 0, 7) * 16 + m[:, None]], 0.0)
    angle = 2 * np.pi * (m[:, None] * (out % 16)[None, :] % 16) / 16
    c = (weight * np.cos(angle)).reshape(2, 128, 128)
    d = (weight * np.sin(angle)).reshape(2, 128, 128)
    real_in = np.concatenate([c, -d], axis=2)
    imag_in = np.concatenate([d, c], axis=2)
    return np.stack([real_in, imag_in], axis=1).reshape(512, 256)


def relayout(v_ref, s_ref):
    for g in range(8):
        for h in range(2):
            x = v_ref[:, :, g * 8 : g * 8 + 8, h * 128 : h * 128 + 128]
            x = x.astype(F32).reshape(32, 8, 128)
            y = jnp.swapaxes(x, 0, 1).astype(BF16)
            for c in range(8):
                s_ref[(g * 8 + c) * 2 + h] = y[c]


def fill_places(pos_ref, oh_ref):
    pos = pos_ref[...]

    def body(i, carry):
        row = lax.broadcasted_iota(jnp.int32, (128, FEEDS), 0) + i * 128
        hit = jnp.where(row == pos, 1.0, 0.0).astype(BF16)
        oh_ref[pl.ds(pl.multiple_of(i * 128, 128), 128), :] = hit
        return carry

    lax.fori_loop(0, 8, body, 0)


def grid_sums(oh_ref, r1_ref, hh_ref, hl_ref):
    xr = r1_ref[:, 0:16, :].reshape(FEEDS, 128)
    xi = r1_ref[:, 16:32, :].reshape(FEEDS, 128)
    x = jnp.concatenate([xr, xi], axis=1)
    re, im = [], []
    for c in range(4):
        g = mm(oh_ref[c * 256 : c * 256 + 256, :], x)
        re.append(g[:, :128])
        im.append(g[:, 128:])
    er, ei = re[0] + re[2], im[0] + im[2]
    fr, fi = re[1] + re[3], im[1] + im[3]
    dr, di = re[0] - re[2], im[0] - im[2]
    gr, gi = re[1] - re[3], im[1] - im[3]
    parts = [(er + fr, ei + fi), (dr + gi, di - gr), (er - fr, ei - fi), (dr - gi, di + gr)]
    for be in range(4):
        hr, hi = parts[be]
        top = jnp.concatenate([hr, hi], axis=1)
        low = jnp.concatenate([hi, -hr], axis=1)
        hh_ref[be], hl_ref[be] = split(jnp.concatenate([top, low], axis=0))


def north_beams(be, hh_ref, hl_ref, a_hi, a_lo, b_ref):
    b_hi, b_lo = hh_ref[be], hl_ref[be]
    res = (mm(a_hi, b_hi) + (mm(a_hi, b_lo) + mm(a_lo, b_hi))).astype(BF16)
    b_ref[pl.ds(be * 8, 8), 0] = res[:, :128].reshape(8, 32, 128)
    b_ref[pl.ds(be * 8, 8), 1] = res[:, 128:].reshape(8, 32, 128)


def fill_spectrum(f_ref):
    def body(i, carry):
        row = lax.broadcasted_iota(jnp.int32, (128, 1024), 0) + i * 128
        lane = lax.broadcasted_iota(jnp.int32, (128, 1024), 1)
        w = (row >> 5) + 1
        steps = w * (lane >> 4) + ((row >> 4) & 1) * 16
        value = jnp.where((row & 15) == (lane & 15), cos_turns(steps, 64), 0.0)
        f_ref[pl.ds(pl.multiple_of(i * 128, 128), 128), :] = value.astype(BF16)
        return carry

    lax.fori_loop(0, 8, body, 0)


def fill_trials(delay_ref, tab_ref):
    dt = jnp.transpose(delay_ref[...].astype(F32)).astype(jnp.int32)
    dd = jnp.concatenate([dt, dt], axis=1)
    rows = []
    for rb in range(32):
        d = (rb // 8) * 4 + (rb // 2) % 4
        rows.append(dd[d * 8 : d * 8 + 8, :])
    step = jnp.concatenate(rows, axis=0)
    row = lax.broadcasted_iota(jnp.int32, (256, 128), 0)
    lane = lax.broadcasted_iota(jnp.int32, (256, 128), 1)
    start = 64 + 16 * (((row >> 3) & 1) - (lane >> 6))

    def body(q, phase):
        for k in range(4):
            phase = phase + step
            tab_ref[q, :, k * 128 : k * 128 + 128] = cos_turns(phase, 64).astype(BF16)
        return phase

    lax.fori_loop(0, 8, body, start)


def fill_inverse(mh_ref, ml_ref):
    for w4 in range(4):
        row = lax.broadcasted_iota(jnp.int32, (128, 512), 0)
        lane = lax.broadcasted_iota(jnp.int32, (128, 512), 1)
        w = (row >> 4) * 4 + w4 + 1
        steps = w * (lane & 63) + ((row >> 3) & 1) * 16
        value = jnp.where((row & 7) == (lane >> 6), cos_turns(steps, 64), 0.0)
        scale = jnp.where(w == FRAMES // 2, 1.0, 2.0) * (1.0 / (FRAMES * math.sqrt(FINE)))
        mh_ref[w4], ml_ref[w4] = split(value * scale)


def power(j, block, c_hi_ref, c_lo_ref, out_ref, cc_ref):
    zero = jnp.zeros((32, 128), BF16)
    cur = [jnp.concatenate([block(t, r) for t in range(8)], axis=0) for r in range(2)]
    old = [jnp.concatenate([zero, cur[r][:224]], axis=0) for r in range(2)]
    left = jnp.concatenate(old + cur, axis=1)
    y = mm(left, c_hi_ref[...]) + mm(left, c_lo_ref[...])
    p = y[:, :128] * y[:, :128] + y[:, 128:] * y[:, 128:]
    total = p[0:32]
    for t in range(1, 8):
        total = total + p[t * 32 : t * 32 + 32]
    for shift in (16, 32, 64):
        total = total + pltpu.roll(total, shift, 1)
    mean = total * (1.0 / FRAMES)
    for t in range(8):
        pt = p[t * 32 : t * 32 + 32]
        out_ref[pl.ds(t * 4 + j, 32, stride=32), :] = pt
        cc_ref[pl.ds(pl.multiple_of(j * 32, 32), 32), t * 128 : t * 128 + 128] = (pt - mean).astype(BF16)


def bin_quad(q, f_ref, cc_ref):
    group = lax.broadcasted_iota(jnp.int32, (16, 128), 1) >> 5
    s = lax.dot_general(
        f_ref[q * 128 : q * 128 + 128, :], cc_ref[...], (((1,), (1,)), ((), ())), preferred_element_type=F32
    )
    turned = [s] + [pltpu.roll(s, 32 * k, 1) for k in range(1, 4)]
    rows = []
    for w4 in range(4):
        for r in range(2):
            for j in range(4):
                at = (w4 * 2 + r) * 16
                part = turned[(w4 - j) % 4][at : at + 16]
                rows.append(jnp.where(group == w4, part, 0.0).astype(BF16))
    return jnp.concatenate(rows, axis=0)


def series(v, mh_ref, ml_ref, out_ref):
    v_hi, v_lo = split(jnp.transpose(v))
    res = jnp.zeros((32, 512), F32)
    for w4 in range(4):
        rows = slice(w4 * 32, w4 * 32 + 32)
        res = res + mm(v_hi[rows], mh_ref[w4]) + (mm(v_lo[rows], mh_ref[w4]) + mm(v_hi[rows], ml_ref[w4]))
    for d in range(8):
        out_ref[pl.ds(d, 32, stride=8), :] = res[:, d * 64 : d * 64 + 64]


MESH = pl.DeviceIdType.MESH


def kernel(
    v_ref, pos_ref, delay_ref, ah_any, al_any, ch_any, cl_any,
    i_out, d_ref,
    i_ref, vbuf, ah, al, ch, cl, s1, r1, oh, hh, hl, b, r2, cc, f, tab, right, mh, ml, z, rx, zz, rz,
    load, send1, recv1, send2, recv2, sendx, recvx, sendz, recvz, wave,
):
    channel, tm, beam = lax.axis_index("channel"), lax.axis_index("tm"), lax.axis_index("beam")
    z_hi, x, z_lo, core = channel >> 2, channel & 3, beam >> 1, beam & 1
    place = z_hi * 4 + z_lo

    loads = [
        pltpu.make_async_copy(src, dst, load.at[n])
        for n, (src, dst) in enumerate([(v_ref, vbuf), (ah_any, ah), (al_any, al), (ch_any, ch), (cl_any, cl)])
    ]
    for copy in loads:
        copy.start()

    def around(to, act):
        for dx in range(4):
            for dc in range(2):
                act(((to >> 2) << 2) + ((x + dx) & 3), ((to & 3) << 1) + ((core + dc) & 1))

    def rings(first, count, act):
        def step(n, carry):
            left = first - n
            far = ((left + 1) >> 1) * (((left & 1) << 1) - 1)
            around((place + far + 16) & 15, act)
            return carry

        lax.fori_loop(0, count, step, 0)

    def here(act):
        for dx in range(4):
            for dc in range(2):
                if dx or dc:
                    act((z_hi << 2) + ((x + dx) & 3), (z_lo << 1) + ((core + dc) & 1))

    barrier = pltpu.get_barrier_semaphore()

    def greet(c, bm):
        pl.semaphore_signal(barrier, inc=1, device_id={"channel": c, "tm": tm, "beam": bm}, device_id_type=MESH)

    rings(8, 8, greet)
    for n in range(1, 4):
        for bm in range(8):
            pl.semaphore_signal(
                barrier, inc=1, device_id={"channel": channel, "tm": (tm + n) & 3, "beam": bm}, device_id_type=MESH
            )
    here(greet)
    loads[0].wait()
    relayout(vbuf, s1)
    pl.semaphore_wait(barrier, 95)
    for n, turn in ((0, 1), (1, 3)):
        to = ((z_hi + turn) & 3) * 4 + x
        pl.semaphore_signal(
            wave.at[n], inc=1, device_id={"channel": to, "tm": tm, "beam": beam}, device_id_type=MESH
        )

    def remote(src, dst, send, recv, c, t, bm):
        return pltpu.make_async_remote_copy(
            src_ref=src, dst_ref=dst, send_sem=send, recv_sem=recv,
            device_id={"channel": c, "tm": t, "beam": bm}, device_id_type=MESH,
        )

    def bulk(src, dst, send, recv):
        return remote(src, dst, send, recv, channel, tm, beam ^ 1)

    feed = beam * 16 + channel

    def hand(c, bm):
        remote(s1.at[c * 8 + bm], r1.at[feed], send1, recv1, c, tm, bm).start()

    rings(6, 2, hand)
    pl.semaphore_wait(wave.at[0], 1)
    pl.semaphore_wait(wave.at[1], 1)
    rings(15, 9, hand)
    rings(4, 4, hand)
    here(hand)
    r1[feed] = s1[channel * 8 + beam]
    fill_places(pos_ref, oh)
    fill_spectrum(f)
    fill_trials(delay_ref, tab)
    fill_inverse(mh, ml)
    for copy in loads[1:]:
        copy.wait()
    first = bulk(s1.at[pl.ds(0, 127)], r1.at[pl.ds(0, 127)], send1, recv1)
    first.wait_recv()

    grid_sums(oh, r1, hh, hl)
    slot = z_lo * 8 + tm * 2 + core
    a_hi, a_lo = ah[...], al[...]

    def pass_on(n):
        be, own = east[n], n == 3
        for dc in range(2):
            for dt in range(4):
                if own and dc == 0 and dt == 0:
                    continue
                co, t = (core + dc) & 1, (tm + dt) & 3
                remote(b.at[be * 8 + co * 4 + t], r2.at[slot], send2, recv2.at[(n + 1) & 3], channel, t, be * 2 + co).start()

    east = [(z_lo + 3 - n) & 3 for n in range(4)]
    for n in range(4):
        north_beams(east[n], hh, hl, a_hi, a_lo, b)
        if n:
            pass_on(n - 1)
    r2[slot] = b[z_lo * 8 + core * 4 + tm]
    pass_on(3)
    for n in (1, 2, 3, 0):
        j = (z_lo + n) & 3
        count = 8 if n else 7
        bulk(b.at[pl.ds(0, count)], r2.at[pl.ds(0, count)], send2, recv2.at[n]).wait_recv()
        power(j, lambda t, r, j=j: r2[j * 8 + t, r], ch, cl, i_ref, cc)

    kept = pltpu.make_async_copy(i_ref, i_out, load.at[5])
    kept.start()

    for q in range(8):
        right[q] = bin_quad(q, f, cc)
    turns = (2, 1, 3, 0)
    for n in range(4):
        to_z = (z_hi + turns[n]) & 3
        rows = pl.ds(pl.multiple_of(to_z * 64, 64), 64)
        for q in range(8):
            z[to_z, :, q] = mm(tab[q, rows, :], right[q]).astype(BF16).reshape(4, 16, 128)
        rx[to_z, x] = z[to_z, x]
        for k in range(1, 4):
            to = (x + k) & 3
            remote(z.at[to_z, to], rx.at[to_z, x], sendx.at[n], recvx.at[n], z_hi * 4 + to, tm, beam).start()

    x_copies = [bulk(z.at[0, pl.ds(0, 3)], rx.at[0, pl.ds(0, 3)], sendx.at[n], recvx.at[n]) for n in range(4)]
    z_copies = [bulk(zz.at[0], rz.at[0], sendz.at[n], recvz.at[n]) for n in range(3)]
    for n in range(4):
        to_z = (z_hi + turns[n]) & 3
        x_copies[n].wait_recv()
        total = rx[to_z, 0].astype(F32)
        for k in range(1, 4):
            total = total + rx[to_z, k].astype(F32)
        if n < 3:
            zz[to_z] = total.astype(BF16)
            remote(zz.at[to_z], rz.at[z_hi], sendz.at[n], recvz.at[n], to_z * 4 + x, tm, beam).start()
        else:
            rz[z_hi] = total.astype(BF16)
    kept.wait()
    first.wait_send()
    bulk(b.at[pl.ds(0, 31)], r2.at[pl.ds(0, 31)], send2, recv2.at[0]).wait_send()
    for copy in x_copies:
        copy.wait_send()
    for copy in z_copies:
        copy.wait_recv()
    total = rz[0].astype(F32)
    for n in range(1, 4):
        total = total + rz[n].astype(F32)
    series(total.reshape(128, 128), mh, ml, d_ref)
    for copy in z_copies:
        copy.wait_send()


def S(shape, dtype):
    return jax.ShapeDtypeStruct(shape, dtype)


def put_out(i_ref, d_ref, i_out, d_out, i_buf, d_buf, sems):
    pairs = [(i_ref.at[pl.ds(n * 256, 256)], i_buf.at[pl.ds(n * 256, 256)], i_out.at[pl.ds(n * 256, 256)]) for n in range(4)]
    pairs.append((d_ref, d_buf, d_out))
    come = [pltpu.make_async_copy(a, b, sems.at[0, n]) for n, (a, b, c) in enumerate(pairs)]
    go = [pltpu.make_async_copy(b, c, sems.at[1, n]) for n, (a, b, c) in enumerate(pairs)]
    for copy in come:
        copy.start()
    for n in range(5):
        come[n].wait()
        go[n].start()
    for copy in go:
        copy.wait()


def per_device(voltages, positions, delays):
    tables = table_split(north_table()) + table_split(filter_table())
    vmem = pl.BlockSpec(memory_space=pltpu.VMEM)
    hbm = pl.BlockSpec(memory_space=pl.ANY)
    V = pltpu.VMEM
    dma = pltpu.SemaphoreType.DMA
    i, d = pl.pallas_call(
        kernel,
        out_shape=[S((1024, 128), F32), S((256, 64), F32)],
        in_specs=[hbm, vmem, vmem] + [hbm] * 4,
        out_specs=[hbm, vmem],
        scratch_shapes=[
            V((1024, 128), F32),
            V((2, 16, 64, 256), BF16),
            V((256, 512), BF16),
            V((256, 512), BF16),
            V((512, 256), BF16),
            V((512, 256), BF16),
            V((128, 32, 128), BF16),
            V((128, 32, 128), BF16),
            V((1024, FEEDS), BF16),
            V((4, 512, 256), BF16),
            V((4, 512, 256), BF16),
            V((32, 2, 32, 128), BF16),
            V((32, 2, 32, 128), BF16),
            V((128, 1024), BF16),
            V((1024, 1024), BF16),
            V((8, 256, 512), BF16),
            V((8, 512, 128), BF16),
            V((4, 128, 512), BF16),
            V((4, 128, 512), BF16),
            V((4, 4, 8, 16, 128), BF16),
            V((4, 4, 8, 16, 128), BF16),
            V((4, 8, 16, 128), BF16),
            V((4, 8, 16, 128), BF16),
            dma((6,)),
            dma,
            dma,
            dma,
            dma((4,)),
            dma((4,)),
            dma((4,)),
            dma((4,)),
            dma((4,)),
            pltpu.SemaphoreType.REGULAR((2,)),
        ],
        compiler_params=pltpu.CompilerParams(collective_id=0, has_side_effects=True, vmem_limit_bytes=60 << 20),
    )(voltages, positions.reshape(1, FEEDS), delays.T, *tables)
    i, d = pl.pallas_call(
        put_out,
        out_shape=[S((1024, 128), F32), S((256, 64), F32)],
        in_specs=[hbm, hbm],
        out_specs=[hbm, hbm],
        scratch_shapes=[V((1024, 128), F32), V((256, 64), F32), dma((2, 5))],
    )(i, d)
    i = i.reshape(32, 8, 4, 128).swapaxes(1, 2).reshape(32, 4, 1024)
    return i, d.reshape(32, 8, 64)


def solution(mesh):
    beam = ("beam", "tm")
    return jax.shard_map(
        per_device,
        mesh=mesh,
        in_specs=(P(None, ("beam", "channel"), None, "tm"), P(), P(None, "channel")),
        out_specs=(P(beam, "channel", None), P(beam, "channel", None)),
        check_vma=False,
    )
```

```python
import math

import jax
import jax.numpy as jnp
import numpy as np
from jax import lax
from jax.experimental import pallas as pl
from jax.experimental.pallas import tpu as pltpu
from jax.sharding import PartitionSpec as P

F32 = jnp.float32
BF16 = jnp.bfloat16
FEEDS = 2048
TAPS = 8
UPCH = 16
FRAMES = 64
FINE = 1024


def cos_turns(steps, period):
    left = (steps & (period - 1)) - period // 2
    u = jnp.abs(left).astype(F32) * (4.0 / period) - 1.0
    u2 = u * u
    p = -3.598843235e-06
    for c in (1.604411848e-04, -4.681754135e-03, 7.969262625e-02, -6.459640975e-01, 1.570796327e00):
        p = p * u2 + c
    return p * u


def split(value):
    high = value.astype(BF16)
    return high, (value - high.astype(F32)).astype(BF16)


def mm(a, b):
    return jnp.dot(a, b, preferred_element_type=F32)


def table_split(table):
    table = jnp.asarray(table.astype(np.float32))
    high = table.astype(BF16)
    return high, (table - high.astype(F32)).astype(BF16)


def north_table():
    n = np.arange(256)
    angle = 2 * np.pi * (n[:, None] * n[None, :] % 256) / 256
    return np.concatenate([np.cos(angle), np.sin(angle)], axis=1) / math.sqrt(FEEDS)


def filter_table():
    length = TAPS * UPCH
    j = np.arange(length)
    h = np.sinc((j - (length - 1) / 2) / UPCH) * (0.5 - 0.5 * np.cos(2 * np.pi * (j + 0.5) / length))
    h = h / np.sqrt(np.sum(h * h))
    s = np.arange(256)
    out = np.arange(128)
    tap = (s[:, None] // 16 - 8) - out[None, :] // 16 + 7
    m = s % 16
    used = (tap >= 0) & (tap < 8)
    weight = np.where(used, h[np.clip(tap, 0, 7) * 16 + m[:, None]], 0.0)
    angle = 2 * np.pi * (m[:, None] * (out % 16)[None, :] % 16) / 16
    c = (weight * np.cos(angle)).reshape(2, 128, 128)
    d = (weight * np.sin(angle)).reshape(2, 128, 128)
    real_in = np.concatenate([c, -d], axis=2)
    imag_in = np.concatenate([d, c], axis=2)
    return np.stack([real_in, imag_in], axis=1).reshape(512, 256)


def relayout(v_ref, s_ref):
    for g in range(8):
        for h in range(2):
            x = v_ref[:, :, g * 8 : g * 8 + 8, h * 128 : h * 128 + 128]
            x = x.astype(F32).reshape(32, 8, 128)
            y = jnp.swapaxes(x, 0, 1).astype(BF16)
            for c in range(8):
                s_ref[(g * 8 + c) * 2 + h] = y[c]


def fill_places(pos_ref, oh_ref):
    pos = pos_ref[...]

    def body(i, carry):
        row = lax.broadcasted_iota(jnp.int32, (128, FEEDS), 0) + i * 128
        hit = jnp.where(row == pos, 1.0, 0.0).astype(BF16)
        oh_ref[pl.ds(pl.multiple_of(i * 128, 128), 128), :] = hit
        return carry

    lax.fori_loop(0, 8, body, 0)


def grid_sums(oh_ref, r1_ref, hh_ref, hl_ref):
    xr = r1_ref[:, 0:16, :].reshape(FEEDS, 128)
    xi = r1_ref[:, 16:32, :].reshape(FEEDS, 128)
    x = jnp.concatenate([xr, xi], axis=1)
    re, im = [], []
    for c in range(4):
        g = mm(oh_ref[c * 256 : c * 256 + 256, :], x)
        re.append(g[:, :128])
        im.append(g[:, 128:])
    er, ei = re[0] + re[2], im[0] + im[2]
    fr, fi = re[1] + re[3], im[1] + im[3]
    dr, di = re[0] - re[2], im[0] - im[2]
    gr, gi = re[1] - re[3], im[1] - im[3]
    parts = [(er + fr, ei + fi), (dr + gi, di - gr), (er - fr, ei - fi), (dr - gi, di + gr)]
    for be in range(4):
        hr, hi = parts[be]
        top = jnp.concatenate([hr, hi], axis=1)
        low = jnp.concatenate([hi, -hr], axis=1)
        hh_ref[be], hl_ref[be] = split(jnp.concatenate([top, low], axis=0))


def north_beams(be, hh_ref, hl_ref, a_hi, a_lo, b_ref):
    b_hi, b_lo = hh_ref[be], hl_ref[be]
    res = (mm(a_hi, b_hi) + (mm(a_hi, b_lo) + mm(a_lo, b_hi))).astype(BF16)
    b_ref[pl.ds(be * 8, 8), 0] = res[:, :128].reshape(8, 32, 128)
    b_ref[pl.ds(be * 8, 8), 1] = res[:, 128:].reshape(8, 32, 128)


def fill_spectrum(f_ref):
    def body(i, carry):
        row = lax.broadcasted_iota(jnp.int32, (128, 1024), 0) + i * 128
        lane = lax.broadcasted_iota(jnp.int32, (128, 1024), 1)
        w = (row >> 5) + 1
        steps = w * (lane >> 4) + ((row >> 4) & 1) * 16
        value = jnp.where((row & 15) == (lane & 15), cos_turns(steps, 64), 0.0)
        f_ref[pl.ds(pl.multiple_of(i * 128, 128), 128), :] = value.astype(BF16)
        return carry

    lax.fori_loop(0, 8, body, 0)


def fill_trials(delay_ref, tab_ref):
    dt = jnp.transpose(delay_ref[...].astype(F32)).astype(jnp.int32)
    dd = jnp.concatenate([dt, dt], axis=1)
    rows = []
    for rb in range(32):
        d = (rb // 8) * 4 + (rb // 2) % 4
        rows.append(dd[d * 8 : d * 8 + 8, :])
    step = jnp.concatenate(rows, axis=0)
    row = lax.broadcasted_iota(jnp.int32, (256, 128), 0)
    lane = lax.broadcasted_iota(jnp.int32, (256, 128), 1)
    start = 64 + 16 * (((row >> 3) & 1) - (lane >> 6))

    def body(q, phase):
        for k in range(4):
            phase = phase + step
            tab_ref[q, :, k * 128 : k * 128 + 128] = cos_turns(phase, 64).astype(BF16)
        return phase

    lax.fori_loop(0, 8, body, start)


def fill_inverse(mh_ref, ml_ref):
    for w4 in range(4):
        row = lax.broadcasted_iota(jnp.int32, (128, 512), 0)
        lane = lax.broadcasted_iota(jnp.int32, (128, 512), 1)
        w = (row >> 4) * 4 + w4 + 1
        steps = w * (lane & 63) + ((row >> 3) & 1) * 16
        value = jnp.where((row & 7) == (lane >> 6), cos_turns(steps, 64), 0.0)
        scale = jnp.where(w == FRAMES // 2, 1.0, 2.0) * (1.0 / (FRAMES * math.sqrt(FINE)))
        mh_ref[w4], ml_ref[w4] = split(value * scale)


def power(j, block, c_hi_ref, c_lo_ref, out_ref, cc_ref):
    zero = jnp.zeros((32, 128), BF16)
    cur = [jnp.concatenate([block(t, r) for t in range(8)], axis=0) for r in range(2)]
    old = [jnp.concatenate([zero, cur[r][:224]], axis=0) for r in range(2)]
    left = jnp.concatenate(old + cur, axis=1)
    y = mm(left, c_hi_ref[...]) + mm(left, c_lo_ref[...])
    p = y[:, :128] * y[:, :128] + y[:, 128:] * y[:, 128:]
    total = p[0:32]
    for t in range(1, 8):
        total = total + p[t * 32 : t * 32 + 32]
    for shift in (16, 32, 64):
        total = total + pltpu.roll(total, shift, 1)
    mean = total * (1.0 / FRAMES)
    for t in range(8):
        pt = p[t * 32 : t * 32 + 32]
        out_ref[pl.ds(t * 4 + j, 32, stride=32), :] = pt
        cc_ref[pl.ds(pl.multiple_of(j * 32, 32), 32), t * 128 : t * 128 + 128] = (pt - mean).astype(BF16)


def bin_quad(q, f_ref, cc_ref):
    group = lax.broadcasted_iota(jnp.int32, (16, 128), 1) >> 5
    s = lax.dot_general(
        f_ref[q * 128 : q * 128 + 128, :], cc_ref[...], (((1,), (1,)), ((), ())), preferred_element_type=F32
    )
    turned = [s] + [pltpu.roll(s, 32 * k, 1) for k in range(1, 4)]
    rows = []
    for w4 in range(4):
        for r in range(2):
            for j in range(4):
                at = (w4 * 2 + r) * 16
                part = turned[(w4 - j) % 4][at : at + 16]
                rows.append(jnp.where(group == w4, part, 0.0).astype(BF16))
    return jnp.concatenate(rows, axis=0)


def series(v, mh_ref, ml_ref, out_ref):
    v_hi, v_lo = split(jnp.transpose(v))
    res = jnp.zeros((32, 512), F32)
    for w4 in range(4):
        rows = slice(w4 * 32, w4 * 32 + 32)
        res = res + mm(v_hi[rows], mh_ref[w4]) + (mm(v_lo[rows], mh_ref[w4]) + mm(v_hi[rows], ml_ref[w4]))
    for d in range(8):
        out_ref[pl.ds(d, 32, stride=8), :] = res[:, d * 64 : d * 64 + 64]


MESH = pl.DeviceIdType.MESH


def kernel(
    v_ref, pos_ref, delay_ref, ah_any, al_any, ch_any, cl_any,
    i_out, d_ref,
    i_ref, vbuf, ah, al, ch, cl, s1, r1, oh, hh, hl, b, r2, cc, f, tab, right, mh, ml, z, rx, zz, rz,
    load, send1, recv1, send2, recv2, sendx, recvx, sendz, recvz, wave,
):
    channel, tm, beam = lax.axis_index("channel"), lax.axis_index("tm"), lax.axis_index("beam")
    z_hi, x, z_lo, core = channel >> 2, channel & 3, beam >> 1, beam & 1
    place = z_hi * 4 + z_lo

    loads = [
        pltpu.make_async_copy(src, dst, load.at[n])
        for n, (src, dst) in enumerate([(v_ref, vbuf), (ah_any, ah), (al_any, al), (ch_any, ch), (cl_any, cl)])
    ]
    for copy in loads:
        copy.start()

    def around(to, act):
        for dx in range(4):
            for dc in range(2):
                act(((to >> 2) << 2) + ((x + dx) & 3), ((to & 3) << 1) + ((core + dc) & 1))

    def rings(first, count, act):
        def step(n, carry):
            left = first - n
            far = ((left + 1) >> 1) * (((left & 1) << 1) - 1)
            around((place + far + 16) & 15, act)
            return carry

        lax.fori_loop(0, count, step, 0)

    def here(act):
        for dx in range(4):
            for dc in range(2):
                if dx or dc:
                    act((z_hi << 2) + ((x + dx) & 3), (z_lo << 1) + ((core + dc) & 1))

    barrier = pltpu.get_barrier_semaphore()

    def greet(c, bm):
        pl.semaphore_signal(barrier, inc=1, device_id={"channel": c, "tm": tm, "beam": bm}, device_id_type=MESH)

    rings(8, 8, greet)
    for n in range(1, 4):
        for bm in range(8):
            pl.semaphore_signal(
                barrier, inc=1, device_id={"channel": channel, "tm": (tm + n) & 3, "beam": bm}, device_id_type=MESH
            )
    here(greet)
    loads[0].wait()
    relayout(vbuf, s1)
    pl.semaphore_wait(barrier, 95)
    for n, turn in ((0, 1), (1, 3)):
        to = ((z_hi + turn) & 3) * 4 + x
        pl.semaphore_signal(
            wave.at[n], inc=1, device_id={"channel": to, "tm": tm, "beam": beam}, device_id_type=MESH
        )

    def remote(src, dst, send, recv, c, t, bm):
        return pltpu.make_async_remote_copy(
            src_ref=src, dst_ref=dst, send_sem=send, recv_sem=recv,
            device_id={"channel": c, "tm": t, "beam": bm}, device_id_type=MESH,
        )

    def bulk(src, dst, send, recv):
        return remote(src, dst, send, recv, channel, tm, beam ^ 1)

    feed = beam * 16 + channel

    def hand(c, bm):
        remote(s1.at[c * 8 + bm], r1.at[feed], send1, recv1, c, tm, bm).start()

    rings(6, 4, hand)
    pl.semaphore_wait(wave.at[0], 1)
    pl.semaphore_wait(wave.at[1], 1)
    rings(15, 9, hand)
    rings(2, 2, hand)
    here(hand)
    r1[feed] = s1[channel * 8 + beam]
    fill_places(pos_ref, oh)
    fill_spectrum(f)
    fill_trials(delay_ref, tab)
    fill_inverse(mh, ml)
    for copy in loads[1:]:
        copy.wait()
    first = bulk(s1.at[pl.ds(0, 127)], r1.at[pl.ds(0, 127)], send1, recv1)
    first.wait_recv()

    grid_sums(oh, r1, hh, hl)
    slot = z_lo * 8 + tm * 2 + core
    a_hi, a_lo = ah[...], al[...]

    def pass_on(n):
        be, own = east[n], n == 3
        for dc in range(2):
            for dt in range(4):
                if own and dc == 0 and dt == 0:
                    continue
                co, t = (core + dc) & 1, (tm + dt) & 3
                remote(b.at[be * 8 + co * 4 + t], r2.at[slot], send2, recv2.at[(n + 1) & 3], channel, t, be * 2 + co).start()

    east = [(z_lo + 3 - n) & 3 for n in range(4)]
    for n in range(4):
        north_beams(east[n], hh, hl, a_hi, a_lo, b)
        if n:
            pass_on(n - 1)
    r2[slot] = b[z_lo * 8 + core * 4 + tm]
    pass_on(3)
    for n in (1, 2, 3, 0):
        j = (z_lo + n) & 3
        count = 8 if n else 7
        bulk(b.at[pl.ds(0, count)], r2.at[pl.ds(0, count)], send2, recv2.at[n]).wait_recv()
        power(j, lambda t, r, j=j: r2[j * 8 + t, r], ch, cl, i_ref, cc)

    kept = pltpu.make_async_copy(i_ref, i_out, load.at[5])
    kept.start()

    for q in range(8):
        right[q] = bin_quad(q, f, cc)
    turns = (2, 1, 3, 0)
    for n in range(4):
        to_z = (z_hi + turns[n]) & 3
        rows = pl.ds(pl.multiple_of(to_z * 64, 64), 64)
        for q in range(8):
            z[to_z, :, q] = mm(tab[q, rows, :], right[q]).astype(BF16).reshape(4, 16, 128)
        rx[to_z, x] = z[to_z, x]
        for k in range(1, 4):
            to = (x + k) & 3
            remote(z.at[to_z, to], rx.at[to_z, x], sendx.at[n], recvx.at[n], z_hi * 4 + to, tm, beam).start()

    x_copies = [bulk(z.at[0, pl.ds(0, 3)], rx.at[0, pl.ds(0, 3)], sendx.at[n], recvx.at[n]) for n in range(4)]
    z_copies = [bulk(zz.at[0], rz.at[0], sendz.at[n], recvz.at[n]) for n in range(3)]
    for n in range(4):
        to_z = (z_hi + turns[n]) & 3
        x_copies[n].wait_recv()
        total = rx[to_z, 0].astype(F32)
        for k in range(1, 4):
            total = total + rx[to_z, k].astype(F32)
        if n < 3:
            zz[to_z] = total.astype(BF16)
            remote(zz.at[to_z], rz.at[z_hi], sendz.at[n], recvz.at[n], to_z * 4 + x, tm, beam).start()
        else:
            rz[z_hi] = total.astype(BF16)
    kept.wait()
    first.wait_send()
    bulk(b.at[pl.ds(0, 31)], r2.at[pl.ds(0, 31)], send2, recv2.at[0]).wait_send()
    for copy in x_copies:
        copy.wait_send()
    for copy in z_copies:
        copy.wait_recv()
    total = rz[0].astype(F32)
    for n in range(1, 4):
        total = total + rz[n].astype(F32)
    series(total.reshape(128, 128), mh, ml, d_ref)
    for copy in z_copies:
        copy.wait_send()


def S(shape, dtype):
    return jax.ShapeDtypeStruct(shape, dtype)


def put_out(i_ref, d_ref, i_out, d_out, i_buf, d_buf, sems):
    pairs = [(i_ref.at[pl.ds(n * 256, 256)], i_buf.at[pl.ds(n * 256, 256)], i_out.at[pl.ds(n * 256, 256)]) for n in range(4)]
    pairs.append((d_ref, d_buf, d_out))
    come = [pltpu.make_async_copy(a, b, sems.at[0, n]) for n, (a, b, c) in enumerate(pairs)]
    go = [pltpu.make_async_copy(b, c, sems.at[1, n]) for n, (a, b, c) in enumerate(pairs)]
    for copy in come:
        copy.start()
    for n in range(5):
        come[n].wait()
        go[n].start()
    for copy in go:
        copy.wait()


def per_device(voltages, positions, delays):
    tables = table_split(north_table()) + table_split(filter_table())
    vmem = pl.BlockSpec(memory_space=pltpu.VMEM)
    hbm = pl.BlockSpec(memory_space=pl.ANY)
    V = pltpu.VMEM
    dma = pltpu.SemaphoreType.DMA
    i, d = pl.pallas_call(
        kernel,
        out_shape=[S((1024, 128), F32), S((256, 64), F32)],
        in_specs=[hbm, vmem, vmem] + [hbm] * 4,
        out_specs=[hbm, vmem],
        scratch_shapes=[
            V((1024, 128), F32),
            V((2, 16, 64, 256), BF16),
            V((256, 512), BF16),
            V((256, 512), BF16),
            V((512, 256), BF16),
            V((512, 256), BF16),
            V((128, 32, 128), BF16),
            V((128, 32, 128), BF16),
            V((1024, FEEDS), BF16),
            V((4, 512, 256), BF16),
            V((4, 512, 256), BF16),
            V((32, 2, 32, 128), BF16),
            V((32, 2, 32, 128), BF16),
            V((128, 1024), BF16),
            V((1024, 1024), BF16),
            V((8, 256, 512), BF16),
            V((8, 512, 128), BF16),
            V((4, 128, 512), BF16),
            V((4, 128, 512), BF16),
            V((4, 4, 8, 16, 128), BF16),
            V((4, 4, 8, 16, 128), BF16),
            V((4, 8, 16, 128), BF16),
            V((4, 8, 16, 128), BF16),
            dma((6,)),
            dma,
            dma,
            dma,
            dma((4,)),
            dma((4,)),
            dma((4,)),
            dma((4,)),
            dma((4,)),
            pltpu.SemaphoreType.REGULAR((2,)),
        ],
        compiler_params=pltpu.CompilerParams(collective_id=0, has_side_effects=True, vmem_limit_bytes=60 << 20),
    )(voltages, positions.reshape(1, FEEDS), delays.T, *tables)
    i, d = pl.pallas_call(
        put_out,
        out_shape=[S((1024, 128), F32), S((256, 64), F32)],
        in_specs=[hbm, hbm],
        out_specs=[hbm, hbm],
        scratch_shapes=[V((1024, 128), F32), V((256, 64), F32), dma((2, 5))],
    )(i, d)
    i = i.reshape(32, 8, 4, 128).swapaxes(1, 2).reshape(32, 4, 1024)
    return i, d.reshape(32, 8, 64)


def solution(mesh):
    beam = ("beam", "tm")
    return jax.shard_map(
        per_device,
        mesh=mesh,
        in_specs=(P(None, ("beam", "channel"), None, "tm"), P(), P(None, "channel")),
        out_specs=(P(beam, "channel", None), P(beam, "channel", None)),
        check_vma=False,
    )
```
